1024 devices in a mesh: dp: 32 (over y, x_hi, core), fsdp: 32 (over x_lo, z).
Axes of the slice: x: 4 (x_hi: 2, x_lo: 2; x = x_hi * 2 + x_lo), y: 8, z: 16, core: 2. Of those that a mesh axis runs over, the one named last changes fastest.
Arguments:
- grads: bfloat16 [32, 1024, 16384], P('dp', None, 'fsdp'), may hold values from -0.44 to 0.44
- stats: float32 [32, 32, 512, 512], P('dp', 'fsdp'), may hold values from -0.08 to 2, as said below
- left_root: bfloat16 [1024, 16384], P(None, 'fsdp'), may hold values from -0.02 to 1, as said below
- right_root: bfloat16 [1024, 16384], P(None, 'fsdp'), may hold values from -1.25 to 1.25, as said below
- owners: int32 [32, 2], replicated, may hold values from 0 to 31, as said below
Outputs:
- update: bfloat16 [1024, 16384], P(None, 'fsdp')
- new_stats: float32 [32, 32, 512, 512], P('dp', 'fsdp')
- new_root: bfloat16 [1024, 16384], P(None, 'fsdp')
The draws below stay inside these ranges and needn't reach their ends.
Inputs may be any that keep to these rules, and one draw needn't show every extreme that they name: `stats`: symmetric in each slot. `left_root`: symmetric in each block. `right_root`: symmetric in each block. `owners`: the 2 entries of each row are distinct.
All inputs are finite; a program needn't handle non-finite values.
Results may differ from the reference program's by a relative error of at most 0.033.
Values may be sent and summed in bfloat16 or wider, within the bound.
No kernel may reach another device: no remote copies, remote signals or barrier semaphores. Data moves between devices by JAX's collectives and lax.ppermute only.
A program may use at most 32 MiB of HBM per device.

```python
import jax
import jax.numpy as jnp
from jax import lax

BLOCK = 512
BLOCK_ROWS = 2
ROWS = 1024
COLS = 16384
N_DP = 32
N_FSDP = 32


def root_draw(key, low, high):
    noise_key = jax.random.fold_in(key, 21)
    diag_key = jax.random.fold_in(key, 22)
    noise = jnp.clip(jax.random.normal(noise_key, (BLOCK_ROWS, BLOCK, N_FSDP, BLOCK)), -6.0, 6.0)
    symmetric = 0.5 * (noise + jnp.transpose(noise, (0, 3, 2, 1)))
    diagonal = jnp.exp(jax.random.uniform(diag_key, (BLOCK_ROWS, BLOCK, N_FSDP), minval=jnp.log(low), maxval=jnp.log(high)))
    identity = jnp.eye(BLOCK, dtype=jnp.float32)[None, :, None, :]
    values = 0.003 * symmetric * (1.0 - identity) + identity * diagonal[..., None]
    return values.reshape(ROWS, COLS).astype(jnp.bfloat16)


def draw_grads(key, part):
    own_key = jax.random.fold_in(key, 1)
    row_key = jax.random.fold_in(key, 3)
    col_key = jax.random.fold_in(key, 4)
    noise = jnp.clip(jax.random.normal(own_key, (N_DP, ROWS, COLS)), -6.0, 6.0)
    row_scale = jnp.exp(jax.random.uniform(row_key, (ROWS,), minval=0.0, maxval=jnp.log(10.0)))
    col_scale = jnp.exp(jax.random.uniform(col_key, (COLS,), minval=0.0, maxval=jnp.log(10.0)))
    ramp = 1.0 + 2.0 * jnp.arange(COLS, dtype=jnp.float32) / (COLS - 1)
    values = 0.0002 * noise * row_scale[None, :, None] * (col_scale * ramp)[None, None, :]
    return values.astype(jnp.bfloat16)


def draw_stats(key, part):
    noise_key = jax.random.fold_in(key, 31)
    diag_key = jax.random.fold_in(key, 32)
    noise = jnp.clip(jax.random.normal(noise_key, (N_DP, N_FSDP, BLOCK, BLOCK)), -6.0, 6.0)
    symmetric = 0.5 * (noise + jnp.swapaxes(noise, 2, 3))
    diagonal = jnp.exp(jax.random.uniform(diag_key, (N_DP, N_FSDP, BLOCK), minval=0.0, maxval=jnp.log(2.0)))
    identity = jnp.eye(BLOCK, dtype=jnp.float32)
    values = 0.012 * symmetric * (1.0 - identity) + identity * diagonal[..., None]
    return values.astype(jnp.float32)


def draw_left_root(key, part):
    return root_draw(jax.random.fold_in(key, 41), 0.84, 1.0)


def draw_right_root(key, part):
    return root_draw(jax.random.fold_in(key, 51), 0.6, 1.2)


def one_permutation(row_key):
    return jax.random.permutation(row_key, N_DP)


def draw_owners(key, part):
    row_keys = jax.random.split(jax.random.fold_in(key, 61), N_FSDP)
    orders = jax.vmap(one_permutation)(row_keys).astype(jnp.int32)
    highest = N_DP - 1
    first_row = orders[0]
    first_row = jnp.where(first_row == highest, first_row[0], first_row).at[0].set(highest)
    second_row = orders[1]
    second_row = jnp.where(second_row == 0, second_row[0], second_row).at[0].set(0)
    orders = orders.at[0].set(first_row).at[1].set(second_row)
    return orders[:, :BLOCK_ROWS].astype(jnp.int32)


def setup_inputs(seed: int = 0) -> dict:
    key_of = jax.random.split(jax.random.key(seed), 6)
    grads = draw_grads(jax.random.fold_in(key_of[5], 71), 0)
    stats = draw_stats(jax.random.fold_in(key_of[5], 71), 0)
    left_root = draw_left_root(jax.random.fold_in(key_of[5], 71), 0)
    right_root = draw_right_root(jax.random.fold_in(key_of[5], 71), 0)
    owners = draw_owners(jax.random.fold_in(key_of[5], 71), 0)
    return dict(grads=grads, stats=stats, left_root=left_root, right_root=right_root, owners=owners)


BETA = 0.95
EPSILON = 1e-06

def precise(left_arg, right_arg):
    return jnp.dot(left_arg, right_arg, preferred_element_type=jnp.float32, precision=lax.Precision.HIGHEST)

def as_blocks(matrix):
    return matrix.reshape(BLOCK_ROWS, BLOCK, N_FSDP, BLOCK).transpose(2, 0, 1, 3).reshape(N_FSDP * BLOCK_ROWS, BLOCK, BLOCK)

def from_blocks(pieces):
    return pieces.reshape(N_FSDP, BLOCK_ROWS, BLOCK, BLOCK).transpose(1, 2, 0, 3).reshape(ROWS, COLS)

def per_block(block_items):
    grad_block, left_block, right_block, old_stats = block_items
    fresh_stats = BETA * old_stats + (1.0 - BETA) * jnp.einsum('ik,jk->ij', grad_block.astype(jnp.float32), grad_block.astype(jnp.float32))
    left_product = jnp.dot(left_block, grad_block, preferred_element_type=jnp.float32).astype(jnp.bfloat16)
    raw_update = jnp.dot(left_product, right_block, preferred_element_type=jnp.float32)
    start_root = left_block.astype(jnp.float32)
    square = precise(start_root, start_root)
    middle = precise(precise(square, fresh_stats), square)
    identity = jnp.eye(BLOCK, dtype=jnp.float32)
    refreshed = precise(start_root, (5.0 * identity - middle) * 0.25).astype(jnp.bfloat16)
    return (fresh_stats, raw_update.astype(jnp.bfloat16), jnp.sum(raw_update * raw_update), refreshed)

def reference(grads, stats, left_root, right_root, owners):
    total_grad = lax.optimization_barrier(jnp.sum(grads.astype(jnp.float32), axis=0))
    summed = total_grad.astype(jnp.bfloat16)
    columns = jnp.arange(N_FSDP, dtype=jnp.int32)[:, None]
    old_stats = stats[owners, columns].reshape(N_FSDP * BLOCK_ROWS, BLOCK, BLOCK)
    fresh_stats, rounded, squares, refreshed = lax.map(per_block, (as_blocks(summed), as_blocks(left_root), as_blocks(right_root), old_stats))
    rms_scale = lax.rsqrt(jnp.sum(squares) / (ROWS * COLS) + EPSILON)
    widened = lax.optimization_barrier(rounded).astype(jnp.float32)
    update = from_blocks((widened * rms_scale).astype(jnp.bfloat16))
    new_stats = jnp.zeros_like(stats).at[owners, columns].set(fresh_stats.reshape(N_FSDP, BLOCK_ROWS, BLOCK, BLOCK))
    new_root = from_blocks(refreshed)
    return (update, new_stats, new_root)
```

```python
import jax
import jax.numpy as jnp
from jax import lax
from jax.sharding import PartitionSpec as P

BETA = 0.95
EPSILON = 1e-06
F32 = jnp.float32
BF16 = jnp.bfloat16


def exchange(array, axis, groups=None):
    return lax.all_to_all(array, axis, 0, 0, axis_index_groups=groups)


def mm(left_arg, right_arg):
    return jnp.dot(left_arg, right_arg, preferred_element_type=F32)


def local(grads, stats, left_root, right_root, owners):
    n_dp = lax.axis_size("dp")
    n_fsdp = lax.axis_size("fsdp")
    chips = n_dp // 2
    width = stats.shape[-1]
    block_rows = left_root.shape[0] // width
    piece = width // chips
    half = piece // 2
    pairs = [[2 * k, 2 * k + 1] for k in range(chips)]
    same_core = [[2 * k + core for k in range(chips)] for core in range(2)]
    replica = lax.axis_index("dp")
    column = lax.axis_index("fsdp")
    owner_row = lax.dynamic_index_in_dim(owners, column, 0, keepdims=False)
    old_stats = stats[0, 0]

    grad_pair = exchange(grads[0].reshape(2, width, width), "dp", pairs)
    stat_pair = exchange(old_stats.astype(BF16).reshape(2, width // 2, width), "dp", pairs)
    grad_part = (grad_pair[0].astype(F32) + grad_pair[1].astype(F32)).astype(BF16)

    stat_pieces = stat_pair.reshape(2, chips, half, width).transpose(1, 0, 2, 3).reshape(chips, piece, width)
    sent = jnp.concatenate([grad_part.reshape(chips, piece, width), stat_pieces], axis=1)
    got = exchange(sent, "dp", same_core)
    grad_piece = jnp.sum(got[:, :piece].astype(F32), axis=0).astype(BF16)
    by_owner = got[:, piece:].reshape(n_dp, half, width)
    stat_piece = [
        lax.dynamic_index_in_dim(by_owner, owner_row[i], 0, keepdims=False) for i in range(block_rows)
    ]

    whole = jnp.concatenate([grad_piece, *stat_piece], axis=0)
    mine = exchange(jnp.broadcast_to(whole[None], (chips, *whole.shape)), "dp", same_core)
    other = lax.ppermute(mine, "dp", [(k, k ^ 1) for k in range(n_dp)])
    first = lax.rem(replica, 2) == 0
    of_core = (jnp.where(first, mine, other), jnp.where(first, other, mine))

    rounded = []
    roots = []
    grams = []
    squares = jnp.zeros((), F32)
    for i in range(block_rows):
        grad_block = of_core[i][:, :piece].reshape(width, width)
        left = left_root[i * width : (i + 1) * width]
        right = right_root[i * width : (i + 1) * width]
        raw = mm(mm(left, grad_block).astype(BF16), right)
        squares = squares + jnp.sum(raw * raw)
        rounded.append(raw.astype(BF16))
        gram = lax.dot_general(grad_block, grad_block, (((1,), (1,)), ((), ())), preferred_element_type=F32)
        grams.append(gram)
        start = piece + i * half
        stat_block = jnp.concatenate(
            [part[:, start : start + half].reshape(width // 2, width) for part in of_core], axis=0
        )
        fresh = (BETA * stat_block.astype(F32) + (1.0 - BETA) * gram).astype(BF16)
        square = mm(left, left).astype(BF16)
        cube = mm(left, square).astype(BF16)
        roots.append(
            (1.25 * left.astype(F32) - 0.25 * mm(cube, mm(fresh, square).astype(BF16))).astype(BF16)
        )

    every = exchange(jnp.broadcast_to(squares, (n_fsdp, 1, 128)), "fsdp")
    total = jnp.sum(every[:, 0, 0])
    scale = lax.rsqrt(total / (left_root.shape[0] * width * n_fsdp) + EPSILON)
    update = jnp.concatenate([(piece_.astype(F32) * scale).astype(BF16) for piece_ in rounded], axis=0)
    new_root = jnp.concatenate(roots, axis=0)
    mine_gram = grams[0]
    has_block = owner_row[0] == replica
    for i in range(1, block_rows):
        mine_gram = jnp.where(owner_row[i] == replica, grams[i], mine_gram)
        has_block = has_block | (owner_row[i] == replica)
    new_stats = jnp.where(has_block, BETA * old_stats + (1.0 - BETA) * mine_gram, 0.0)
    return (update, new_stats[None, None], new_root)


def solution(mesh):
    in_specs = (
        P("dp", None, "fsdp"),
        P("dp", "fsdp", None, None),
        P(None, "fsdp"),
        P(None, "fsdp"),
        P(),
    )
    out_specs = (P(None, "fsdp"), P("dp", "fsdp", None, None), P(None, "fsdp"))
    return jax.shard_map(local, mesh=mesh, in_specs=in_specs, out_specs=out_specs, check_vma=False)
```

```python
import jax
import jax.numpy as jnp
from jax import lax
from jax.experimental import pallas as pl
from jax.experimental.pallas import tpu as pltpu
from jax.sharding import PartitionSpec as P

BETA = 0.95
EPSILON = 1e-06
F32 = jnp.float32
BF16 = jnp.bfloat16

WIDTH = 512
HALF = 256
TILE = 128
SLOT = 32
CHIPS = 16
N_DP = 32
FIRST = TILE + 2 * SLOT + 16
SECOND = TILE + 2 * SLOT


def exchange(array, axis, groups=None):
    return lax.all_to_all(array, axis, 0, 0, axis_index_groups=groups)


def mm(left_arg, right_arg):
    return jnp.dot(left_arg, right_arg, preferred_element_type=F32)


def row_col(rows, cols):
    shape = (rows, cols)
    return lax.broadcasted_iota(jnp.int32, shape, 0), lax.broadcasted_iota(jnp.int32, shape, 1)


def call(body, meta, args, outs, flops, scratch=()):
    vmem = pl.BlockSpec(memory_space=pltpu.VMEM)
    moved = sum(a.size * a.dtype.itemsize for a in args) + sum(o.size * o.dtype.itemsize for o in outs)
    return pl.pallas_call(
        body,
        out_shape=outs,
        in_specs=[pl.BlockSpec(memory_space=pltpu.SMEM)] + [vmem] * len(args),
        out_specs=[vmem] * len(outs),
        scratch_shapes=scratch,
        cost_estimate=pl.CostEstimate(flops=flops, bytes_accessed=moved, transcendentals=0),
        compiler_params=pltpu.CompilerParams(vmem_limit_bytes=16 << 20),
    )(meta, *args)


def pack(meta, grads, stats, send, keep):
    core = meta[0]
    other = 1 - core
    send[0:WIDTH] = grads[0, pl.ds(pl.multiple_of(other * WIDTH, WIDTH), WIDTH)]
    row, col = row_col(HALF, HALF)
    low = stats[0, 0, HALF:, HALF:]
    both = jnp.where(row <= col, stats[0, 0, :HALF, :HALF], low).astype(BF16)
    corner = stats[0, 0, :HALF, HALF:].astype(BF16)
    diagonal = jnp.sum(jnp.where(row == col, low, 0.0), axis=0, keepdims=True)
    line, _ = row_col(16, TILE)
    lines = jnp.where(line == 8 * core, diagonal[:, :TILE], jnp.where(line == 8 * core + 1, diagonal[:, TILE:], 0.0))
    lines = lines.astype(BF16)

    @pl.when(core == 0)
    def _():
        keep[0:TILE, :HALF] = corner[:TILE]
        keep[0:TILE, HALF:] = both[:TILE]
        send[WIDTH : WIDTH + TILE, :HALF] = corner[TILE:]
        send[WIDTH : WIDTH + TILE, HALF:] = both[TILE:]

    @pl.when(core == 1)
    def _():
        keep[0:TILE, :HALF] = corner[TILE:]
        keep[0:TILE, HALF:] = both[TILE:]
        send[WIDTH : WIDTH + TILE, :HALF] = corner[:TILE]
        send[WIDTH : WIDTH + TILE, HALF:] = both[:TILE]

    for start in range(0, WIDTH, TILE):
        keep[TILE:, start : start + TILE] = lines
        send[WIDTH + TILE :, start : start + TILE] = lines


def pair_add(meta, grads, keep, got, out):
    core = meta[0]
    base = core * WIDTH
    mine = pl.multiple_of(TILE + SLOT * core, SLOT)
    theirs = pl.multiple_of(TILE + SLOT * (1 - core), SLOT)
    lines = (keep[TILE:, :TILE].astype(F32) + got[WIDTH + TILE :, :TILE].astype(F32)).astype(BF16)
    for chip in range(CHIPS):
        cols = slice(TILE * (chip // 4), TILE * (chip // 4) + TILE)
        top = TILE * (chip % 4)
        own = grads[0, pl.ds(pl.multiple_of(base + top, TILE), TILE), cols].astype(F32)
        out[chip, 0:TILE] = (own + got[top : top + TILE, cols].astype(F32)).astype(BF16)
        at = SLOT * (chip % 4)
        out[chip, pl.ds(mine, SLOT)] = keep[at : at + SLOT, cols]
        out[chip, pl.ds(theirs, SLOT)] = got[WIDTH + at : WIDTH + at + SLOT, cols]
        out[chip, SECOND:] = lines


def gather_sum(meta, got, out, diagonals):
    total = got[0, 0:TILE].astype(F32)
    for chip in range(1, CHIPS):
        total = total + got[chip, 0:TILE].astype(F32)
    total = total.astype(BF16)
    line, _ = row_col(16, TILE)
    lines = jnp.zeros((16, TILE), F32)
    slots = []
    for i in range(2):
        owner = meta[1 + i]
        chip = owner // 2
        side = owner % 2
        slots.append(got[chip, pl.ds(pl.multiple_of(TILE + SLOT * side, SLOT), SLOT)])
        rows = got[chip, SECOND:].astype(F32)
        pick = jnp.where(side == 0, rows[0:8], rows[8:16])
        lines = jnp.where(line == 8 * i, pick[0:1], jnp.where(line == 8 * i + 1, pick[1:2], lines))
    diagonals[...] = lines
    for chip in range(CHIPS):
        out[chip, 0:TILE] = total
        for i in range(2):
            out[chip, TILE + SLOT * i : TILE + SLOT * (i + 1)] = slots[i]


def load_grad(source, grad):
    for chip in range(CHIPS):
        top = TILE * (chip % 4)
        left = TILE * (chip // 4)
        grad[top : top + TILE, left : left + TILE] = source[chip, 0:TILE]


def precondition(meta, mine, other, left_root, right_root, rounded, squares, grad):
    core = meta[0]
    total = jnp.zeros((1, 1), F32)
    for source, block in ((mine, core), (other, 1 - core)):
        rows = pl.ds(pl.multiple_of(block * WIDTH, WIDTH), WIDTH)
        load_grad(source, grad)
        product = mm(left_root[rows, :], grad[...]).astype(BF16)
        raw = mm(product, right_root[rows, :])
        rounded[rows, :] = raw.astype(BF16)
        column = jnp.sum(raw * raw, axis=0, keepdims=True)
        total = total + jnp.sum(column, axis=1, keepdims=True)
    filled = jnp.broadcast_to(total, squares.shape[1:])
    for k in range(squares.shape[0]):
        squares[k] = filled


def newton(meta, mine, other, diagonals, left_root, stats, squares, new_root, new_stats, grad):
    core = meta[0]
    owner_known = (meta[1] == meta[3]) | (meta[2] == meta[3])
    row, col = row_col(HALF, HALF)

    @pl.when(jnp.logical_not(owner_known))
    def _():
        new_stats[...] = jnp.zeros_like(new_stats)

    def one(block, source, first, second):
        rows = slice(block * WIDTH, (block + 1) * WIDTH)
        load_grad(source, grad)
        gram = lax.dot_general(
            grad[...], grad[...], (((1,), (1,)), ((), ())), preferred_element_type=F32
        )

        @pl.when(meta[1 + block] == meta[3])
        def _():
            new_stats[0, 0] = BETA * stats[0, 0] + (1.0 - BETA) * gram

        start = TILE + SLOT * block

        def panel(part, k):
            return part[4 * k : 4 * k + 4, start : start + SLOT].reshape(TILE, TILE)

        packed = [
            jnp.concatenate(
                [jnp.concatenate([panel(part, k), panel(part, k + 1)], axis=1) for part in (first, second)], axis=0
            ).astype(F32)
            for k in (0, 2)
        ]
        corner, both = packed
        corner_t = jnp.transpose(corner)
        both_t = jnp.transpose(both)
        diagonal = jnp.concatenate(
            [diagonals[8 * block : 8 * block + 1], diagonals[8 * block + 1 : 8 * block + 2]], axis=1
        )
        high = jnp.where(row <= col, both, both_t)
        low = jnp.where(row > col, both, jnp.where(row == col, diagonal, both_t))
        old = jnp.concatenate(
            [jnp.concatenate([high, corner], axis=1), jnp.concatenate([corner_t, low], axis=1)], axis=0
        )
        fresh = (BETA * old + (1.0 - BETA) * gram).astype(BF16)
        left = left_root[rows, :]
        square = mm(left, left).astype(BF16)
        cube = mm(left, square).astype(BF16)
        change = mm(cube, mm(fresh, square).astype(BF16))
        new_root[rows, :] = (1.25 * left.astype(F32) - 0.25 * change).astype(BF16)

    @pl.when(core == 0)
    def _():
        one(0, mine, mine, other)
        one(1, other, mine, other)

    @pl.when(core == 1)
    def _():
        one(0, other, other, mine)
        one(1, mine, other, mine)


def rescale(count):
    def body(meta, every, rounded, update):
        total = every[0]
        for k in range(1, every.shape[0]):
            total = total + every[k]
        scale = lax.rsqrt(total[0:1, 0:1] / count + EPSILON)
        update[...] = (rounded[...].astype(F32) * scale).astype(BF16)

    return body


def local(grads, stats, left_root, right_root, owners):
    n_fsdp = lax.axis_size("fsdp")
    rows = left_root.shape[0]
    same_core = [[2 * k + core for k in range(CHIPS)] for core in range(2)]
    swap = [(k, k ^ 1) for k in range(N_DP)]
    replica = lax.axis_index("dp")
    column = lax.axis_index("fsdp")
    owner_row = lax.dynamic_index_in_dim(owners, column, 0, keepdims=False)
    meta = jnp.stack([lax.rem(replica, 2), owner_row[0], owner_row[1], replica]).astype(jnp.int32)
    shape = jax.ShapeDtypeStruct
    product = 2 * WIDTH**3

    send, keep = call(
        pack,
        meta,
        [grads, stats],
        [shape((WIDTH + TILE + 16, WIDTH), BF16), shape((TILE + 16, WIDTH), BF16)],
        1 << 20,
    )
    got = lax.ppermute(send, "dp", swap)
    (payload,) = call(pair_add, meta, [grads, keep, got], [shape((CHIPS, FIRST, TILE), BF16)], 1 << 20)
    arrived = exchange(payload, "dp", same_core)
    repeated, diagonals = call(
        gather_sum,
        meta,
        [arrived],
        [shape((CHIPS, SECOND, TILE), BF16), shape((16, TILE), F32)],
        1 << 20,
    )
    mine = exchange(repeated, "dp", same_core)
    other = lax.ppermute(mine, "dp", swap)
    rounded, squares = call(
        precondition,
        meta,
        [mine, other, left_root, right_root],
        [shape((rows, WIDTH), BF16), shape((n_fsdp, 8, TILE), F32)],
        4 * product,
        [pltpu.VMEM((WIDTH, WIDTH), BF16)],
    )
    every = exchange(squares, "fsdp")
    new_root, new_stats = call(
        newton,
        meta,
        [mine, other, diagonals, left_root, stats, squares],
        [shape((rows, WIDTH), BF16), shape((1, 1, WIDTH, WIDTH), F32)],
        10 * product,
        [pltpu.VMEM((WIDTH, WIDTH), BF16)],
    )
    (update,) = call(rescale(float(rows * WIDTH * n_fsdp)), meta, [every, rounded], [shape((rows, WIDTH), BF16)], 1 << 20)
    return (update, new_stats, new_root)


def solution(mesh):
    in_specs = (
        P("dp", None, "fsdp"),
        P("dp", "fsdp", None, None),
        P(None, "fsdp"),
        P(None, "fsdp"),
        P(),
    )
    out_specs = (P(None, "fsdp"), P("dp", "fsdp", None, None), P(None, "fsdp"))
    return jax.shard_map(local, mesh=mesh, in_specs=in_specs, out_specs=out_specs, check_vma=False)
```

```python
import jax
import jax.numpy as jnp
from jax import lax
from jax.experimental import pallas as pl
from jax.experimental.pallas import tpu as pltpu
from jax.sharding import PartitionSpec as P

BETA = 0.95
EPSILON = 1e-06
F32 = jnp.float32
BF16 = jnp.bfloat16

WIDTH = 512
HALF = 256
TILE = 128
SLOT = 32
CHIPS = 16
N_DP = 32
FIRST = TILE + 2 * SLOT + 8
SECOND = TILE + 2 * SLOT


def exchange(array, axis, groups=None):
    return lax.all_to_all(array, axis, 0, 0, axis_index_groups=groups)


def mm(left_arg, right_arg):
    return jnp.dot(left_arg, right_arg, preferred_element_type=F32)


def row_col(rows, cols):
    shape = (rows, cols)
    return lax.broadcasted_iota(jnp.int32, shape, 0), lax.broadcasted_iota(jnp.int32, shape, 1)


def core_of():
    return lax.rem(lax.axis_index("dp"), 2)


def call(body, args, outs, flops, scratch=(), spaces=None, out_spaces=None):
    spaces = spaces or [pltpu.VMEM] * len(args)
    out_spaces = out_spaces or [pltpu.VMEM] * len(outs)
    moved = sum(a.size * a.dtype.itemsize for a in args) + sum(o.size * o.dtype.itemsize for o in outs)
    return pl.pallas_call(
        body,
        out_shape=outs,
        in_specs=[pl.BlockSpec(memory_space=space) for space in spaces],
        out_specs=[pl.BlockSpec(memory_space=space) for space in out_spaces],
        scratch_shapes=scratch,
        cost_estimate=pl.CostEstimate(flops=flops, bytes_accessed=moved, transcendentals=0),
        compiler_params=pltpu.CompilerParams(vmem_limit_bytes=16 << 20),
    )(*args)


def pack(grads, stats, send, keep, upper, lower, sems):
    core = core_of()
    other = 1 - core
    copies = [
        pltpu.make_async_copy(stats.at[0, 0, 0:TILE], upper.at[0:TILE], sems.at[0]),
        pltpu.make_async_copy(stats.at[0, 0, TILE:HALF], upper.at[TILE:HALF], sems.at[1]),
        pltpu.make_async_copy(stats.at[0, 0, HALF:, HALF:], lower, sems.at[2]),
    ]
    for part in range(2):
        for k, (block, target) in enumerate(((other, send), (core, keep))):
            source = grads.at[0, pl.ds(pl.multiple_of(block * WIDTH + part * HALF, HALF), HALF)]
            copies.append(
                pltpu.make_async_copy(source, target.at[part * HALF : part * HALF + HALF], sems.at[3 + 2 * part + k])
            )
    for copy in copies:
        copy.start()
    for copy in copies[:3]:
        copy.wait()
    row, col = row_col(HALF, HALF)
    low = lower[...]
    both = jnp.where(row <= col, upper[:, :HALF], low).astype(BF16)
    corner = upper[:, HALF:].astype(BF16)
    diagonal = jnp.sum(jnp.where(row == col, low, 0.0), axis=0, keepdims=True)
    line, _ = row_col(16, TILE)
    lines = jnp.where(line == 2 * core, diagonal[:, :TILE], jnp.where(line == 2 * core + 1, diagonal[:, TILE:], 0.0))
    lines = lines.astype(BF16)
    end = WIDTH + TILE

    @pl.when(core == 0)
    def _():
        keep[WIDTH:end, :HALF] = corner[:TILE]
        keep[WIDTH:end, HALF:] = both[:TILE]
        send[WIDTH:end, :HALF] = corner[TILE:]
        send[WIDTH:end, HALF:] = both[TILE:]

    @pl.when(core == 1)
    def _():
        keep[WIDTH:end, :HALF] = corner[TILE:]
        keep[WIDTH:end, HALF:] = both[TILE:]
        send[WIDTH:end, :HALF] = corner[:TILE]
        send[WIDTH:end, HALF:] = both[:TILE]

    for start in range(0, WIDTH, TILE):
        keep[end:, start : start + TILE] = lines
        send[end:, start : start + TILE] = lines
    for copy in copies[3:]:
        copy.wait()


def pair_add(keep, got, out):
    core = core_of()
    mine = pl.multiple_of(TILE + SLOT * core, SLOT)
    theirs = pl.multiple_of(TILE + SLOT * (1 - core), SLOT)
    lines = (keep[WIDTH + TILE :, :TILE].astype(F32) + got[WIDTH + TILE :, :TILE].astype(F32))[0:8].astype(BF16)
    for chip in range(CHIPS):
        cols = slice(TILE * (chip // 4), TILE * (chip // 4) + TILE)
        top = TILE * (chip % 4)
        own = keep[top : top + TILE, cols].astype(F32)
        out[chip, 0:TILE] = (own + got[top : top + TILE, cols].astype(F32)).astype(BF16)
        at = WIDTH + SLOT * (chip % 4)
        out[chip, pl.ds(mine, SLOT)] = keep[at : at + SLOT, cols]
        out[chip, pl.ds(theirs, SLOT)] = got[at : at + SLOT, cols]
        out[chip, SECOND:] = lines


def gather_sum(owners, got, out, diagonals):
    column = lax.axis_index("fsdp")
    total = got[0, 0:TILE].astype(F32)
    for chip in range(1, CHIPS):
        total = total + got[chip, 0:TILE].astype(F32)
    total = total.astype(BF16)
    line, _ = row_col(16, TILE)
    lines = jnp.zeros((16, TILE), F32)
    slots = []
    for i in range(2):
        owner = owners[column, i]
        chip = owner // 2
        side = owner % 2
        slots.append(got[chip, pl.ds(pl.multiple_of(TILE + SLOT * side, SLOT), SLOT)])
        rows = got[chip, SECOND:].astype(F32)
        for k in range(2):
            pick = jnp.where(side == 0, rows[k : k + 1], rows[2 + k : 3 + k])
            lines = jnp.where(line == 8 * i + k, pick, lines)
    diagonals[...] = lines
    for chip in range(CHIPS):
        out[chip, 0:TILE] = total
        for i in range(2):
            out[chip, TILE + SLOT * i : TILE + SLOT * (i + 1)] = slots[i]


def load_grad(source, grad):
    for chip in range(CHIPS):
        top = TILE * (chip % 4)
        left = TILE * (chip // 4)
        grad[top : top + TILE, left : left + TILE] = source[chip, 0:TILE]


def precondition(source, left_root, right_root, rounded, grad, block):
    rows = pl.ds(pl.multiple_of(block * WIDTH, WIDTH), WIDTH)
    load_grad(source, grad)
    product = mm(left_root[rows, :], grad[...]).astype(BF16)
    raw = mm(product, right_root[rows, :])
    rounded[...] = raw.astype(BF16)
    column = jnp.sum(raw * raw, axis=0, keepdims=True)
    return jnp.sum(column, axis=1, keepdims=True)


def own_block(mine, left_root, right_root, rounded, squares, grad):
    total = precondition(mine, left_root, right_root, rounded, grad, core_of())
    squares[...] = jnp.broadcast_to(total, squares.shape)


def other_block(other, left_root, right_root, own, rounded, squares, grad):
    total = precondition(other, left_root, right_root, rounded, grad, 1 - core_of())
    filled = own[0:1] + jnp.broadcast_to(total, (1, TILE))
    for k in range(squares.shape[0]):
        squares[k] = filled


def newton(owners, mine, other, diagonals, left_root, stats, squares, new_root, new_stats, grad, old_stats, sem):
    core = core_of()
    replica = lax.axis_index("dp")
    column = lax.axis_index("fsdp")
    fetch = pltpu.make_async_copy(stats.at[0, 0], old_stats, sem)
    fetch.start()
    owner_known = (owners[column, 0] == replica) | (owners[column, 1] == replica)
    row, col = row_col(HALF, HALF)

    @pl.when(jnp.logical_not(owner_known))
    def _():
        new_stats[...] = jnp.zeros_like(new_stats)

    fetch.wait()

    def one(block, source, first, second):
        rows = slice(block * WIDTH, (block + 1) * WIDTH)
        load_grad(source, grad)
        gram = lax.dot_general(
            grad[...], grad[...], (((1,), (1,)), ((), ())), preferred_element_type=F32
        )

        @pl.when(owners[column, block] == replica)
        def _():
            new_stats[0, 0] = BETA * old_stats[...] + (1.0 - BETA) * gram

        start = TILE + SLOT * block

        def panel(part, k):
            return part[4 * k : 4 * k + 4, start : start + SLOT].reshape(TILE, TILE)

        packed = [
            jnp.concatenate(
                [jnp.concatenate([panel(part, k), panel(part, k + 1)], axis=1) for part in (first, second)], axis=0
            ).astype(F32)
            for k in (0, 2)
        ]
        corner, both = packed
        corner_t = jnp.transpose(corner)
        both_t = jnp.transpose(both)
        diagonal = jnp.concatenate(
            [diagonals[8 * block : 8 * block + 1], diagonals[8 * block + 1 : 8 * block + 2]], axis=1
        )
        high = jnp.where(row <= col, both, both_t)
        low = jnp.where(row > col, both, jnp.where(row == col, diagonal, both_t))
        old = jnp.concatenate(
            [jnp.concatenate([high, corner], axis=1), jnp.concatenate([corner_t, low], axis=1)], axis=0
        )
        fresh = (BETA * old + (1.0 - BETA) * gram).astype(BF16)
        left = left_root[rows, :]
        square = mm(left, left).astype(BF16)
        cube = mm(left, square).astype(BF16)
        change = mm(cube, mm(fresh, square).astype(BF16))
        new_root[rows, :] = (1.25 * left.astype(F32) - 0.25 * change).astype(BF16)

    @pl.when(core == 0)
    def _():
        one(0, mine, mine, other)
        one(1, other, mine, other)

    @pl.when(core == 1)
    def _():
        one(0, other, other, mine)
        one(1, mine, other, mine)


def rescale(count):
    def body(every, own, other, update, buffer, sems):
        core = core_of()
        total = every[0]
        for k in range(1, every.shape[0]):
            total = total + every[k]
        scale = lax.rsqrt(total[:, 0:1] / count + EPSILON)
        copies = []
        for source, block in ((own, core), (other, 1 - core)):
            for start in range(0, WIDTH, TILE):
                k = len(copies)
                buffer[k] = (source[start : start + TILE].astype(F32) * scale).astype(BF16)
                to = update.at[pl.ds(pl.multiple_of(block * WIDTH + start, TILE), TILE)]
                copies.append(pltpu.make_async_copy(buffer.at[k], to, sems.at[k]))
                copies[-1].start()
        for copy in copies:
            copy.wait()

    return body


def local(grads, stats, left_root, right_root, owners):
    n_fsdp = lax.axis_size("fsdp")
    rows = left_root.shape[0]
    same_core = [[2 * k + core for k in range(CHIPS)] for core in range(2)]
    swap = [(k, k ^ 1) for k in range(N_DP)]
    shape = jax.ShapeDtypeStruct
    product = 2 * WIDTH**3
    vmem = pltpu.VMEM
    grads, stats = [pltpu.with_memory_space_constraint(array, pltpu.HBM) for array in (grads, stats)]
    block = vmem((WIDTH, WIDTH), BF16)
    packed = WIDTH + TILE + 16

    send, keep = call(
        pack,
        [grads, stats],
        [shape((packed, WIDTH), BF16), shape((packed, WIDTH), BF16)],
        1 << 20,
        [vmem((HALF, WIDTH), F32), vmem((HALF, HALF), F32), pltpu.SemaphoreType.DMA((7,))],
        [pltpu.HBM, pltpu.HBM],
    )
    got = lax.ppermute(send, "dp", swap)
    (payload,) = call(pair_add, [keep, got], [shape((CHIPS, FIRST, TILE), BF16)], 1 << 20)
    arrived = exchange(payload, "dp", same_core)
    repeated, diagonals = call(
        gather_sum,
        [owners, arrived],
        [shape((CHIPS, SECOND, TILE), BF16), shape((16, TILE), F32)],
        1 << 20,
        spaces=[pltpu.SMEM, vmem],
    )
    mine = exchange(repeated, "dp", same_core)
    other = lax.ppermute(mine, "dp", swap)
    own_rounded, own_squares = call(
        own_block,
        [mine, left_root, right_root],
        [shape((WIDTH, WIDTH), BF16), shape((8, TILE), F32)],
        2 * product,
        [block],
    )
    other_rounded, squares = call(
        other_block,
        [other, left_root, right_root, own_squares],
        [shape((WIDTH, WIDTH), BF16), shape((n_fsdp, 1, TILE), F32)],
        2 * product,
        [block],
    )
    every = exchange(squares, "fsdp")
    new_root, new_stats = call(
        newton,
        [owners, mine, other, diagonals, left_root, stats, squares],
        [shape((rows, WIDTH), BF16), shape((1, 1, WIDTH, WIDTH), F32)],
        10 * product,
        [block, vmem((WIDTH, WIDTH), F32), pltpu.SemaphoreType.DMA],
        [pltpu.SMEM, vmem, vmem, vmem, vmem, pltpu.HBM, vmem],
    )
    (update,) = call(
        rescale(float(rows * WIDTH * n_fsdp)),
        [every, own_rounded, other_rounded],
        [shape((rows, WIDTH), BF16)],
        1 << 20,
        [vmem((8, TILE, WIDTH), BF16), pltpu.SemaphoreType.DMA((8,))],
        out_spaces=[pltpu.HBM],
    )
    return (update, new_stats, new_root)


def solution(mesh):
    in_specs = (
        P("dp", None, "fsdp"),
        P("dp", "fsdp", None, None),
        P(None, "fsdp"),
        P(None, "fsdp"),
        P(),
    )
    out_specs = (P(None, "fsdp"), P("dp", "fsdp", None, None), P(None, "fsdp"))
    return jax.shard_map(local, mesh=mesh, in_specs=in_specs, out_specs=out_specs, check_vma=False)
```

```python
import jax
import jax.numpy as jnp
from jax import lax
from jax.experimental import pallas as pl
from jax.experimental.pallas import tpu as pltpu
from jax.sharding import PartitionSpec as P

BETA = 0.95
EPSILON = 1e-06
F32 = jnp.float32
BF16 = jnp.bfloat16

WIDTH = 512
HALF = 256
TILE = 128
SLOT = 32
CHIPS = 16
N_DP = 32
FIRST = TILE + 2 * SLOT + 8
SECOND = TILE + 2 * SLOT


def exchange(array, axis, groups=None):
    return lax.all_to_all(array, axis, 0, 0, axis_index_groups=groups)


def mm(left_arg, right_arg):
    return jnp.dot(left_arg, right_arg, preferred_element_type=F32)


def row_col(rows, cols):
    shape = (rows, cols)
    return lax.broadcasted_iota(jnp.int32, shape, 0), lax.broadcasted_iota(jnp.int32, shape, 1)


def core_of():
    return lax.rem(lax.axis_index("dp"), 2)


def call(body, args, outs, flops, scratch=(), spaces=None, out_spaces=None):
    spaces = spaces or [pltpu.VMEM] * len(args)
    out_spaces = out_spaces or [pltpu.VMEM] * len(outs)
    moved = sum(a.size * a.dtype.itemsize for a in args) + sum(o.size * o.dtype.itemsize for o in outs)
    return pl.pallas_call(
        body,
        out_shape=outs,
        in_specs=[pl.BlockSpec(memory_space=space) for space in spaces],
        out_specs=[pl.BlockSpec(memory_space=space) for space in out_spaces],
        scratch_shapes=scratch,
        cost_estimate=pl.CostEstimate(flops=flops, bytes_accessed=moved, transcendentals=0),
        compiler_params=pltpu.CompilerParams(vmem_limit_bytes=16 << 20),
    )(*args)


def pack(grads, stats, send, keep, upper, lower, sems):
    core = core_of()
    other = 1 - core
    copies = [
        pltpu.make_async_copy(stats.at[0, 0, 0:TILE], upper.at[0:TILE], sems.at[0]),
        pltpu.make_async_copy(stats.at[0, 0, TILE:HALF], upper.at[TILE:HALF], sems.at[1]),
        pltpu.make_async_copy(stats.at[0, 0, HALF:, HALF:], lower, sems.at[2]),
    ]
    for part in range(2):
        for k, (block, target) in enumerate(((other, send), (core, keep))):
            source = grads.at[0, pl.ds(pl.multiple_of(block * WIDTH + part * HALF, HALF), HALF)]
            copies.append(
                pltpu.make_async_copy(source, target.at[part * HALF : part * HALF + HALF], sems.at[3 + 2 * part + k])
            )
    for copy in copies:
        copy.start()
    for copy in copies[:3]:
        copy.wait()
    row, col = row_col(HALF, HALF)
    low = lower[...]
    both = jnp.where(row <= col, upper[:, :HALF], low).astype(BF16)
    corner = upper[:, HALF:].astype(BF16)
    diagonal = jnp.sum(jnp.where(row == col, low, 0.0), axis=0, keepdims=True)
    line, _ = row_col(16, TILE)
    lines = jnp.where(line == 2 * core, diagonal[:, :TILE], jnp.where(line == 2 * core + 1, diagonal[:, TILE:], 0.0))
    lines = lines.astype(BF16)
    end = WIDTH + TILE

    @pl.when(core == 0)
    def _():
        keep[WIDTH:end, :HALF] = corner[:TILE]
        keep[WIDTH:end, HALF:] = both[:TILE]
        send[WIDTH:end, :HALF] = corner[TILE:]
        send[WIDTH:end, HALF:] = both[TILE:]

    @pl.when(core == 1)
    def _():
        keep[WIDTH:end, :HALF] = corner[TILE:]
        keep[WIDTH:end, HALF:] = both[TILE:]
        send[WIDTH:end, :HALF] = corner[:TILE]
        send[WIDTH:end, HALF:] = both[:TILE]

    for start in range(0, WIDTH, TILE):
        keep[end:, start : start + TILE] = lines
        send[end:, start : start + TILE] = lines
    for copy in copies[3:]:
        copy.wait()


def pair_add(keep, got, out):
    core = core_of()
    mine = pl.multiple_of(TILE + SLOT * core, SLOT)
    theirs = pl.multiple_of(TILE + SLOT * (1 - core), SLOT)
    lines = (keep[WIDTH + TILE :, :TILE].astype(F32) + got[WIDTH + TILE :, :TILE].astype(F32))[0:8].astype(BF16)
    for chip in range(CHIPS):
        cols = slice(TILE * (chip // 4), TILE * (chip // 4) + TILE)
        top = TILE * (chip % 4)
        own = keep[top : top + TILE, cols].astype(F32)
        out[chip, 0:TILE] = (own + got[top : top + TILE, cols].astype(F32)).astype(BF16)
        at = WIDTH + SLOT * (chip % 4)
        out[chip, pl.ds(mine, SLOT)] = keep[at : at + SLOT, cols]
        out[chip, pl.ds(theirs, SLOT)] = got[at : at + SLOT, cols]
        out[chip, SECOND:] = lines


def gather_sum(owners, got, out, diagonals):
    column = lax.axis_index("fsdp")
    total = got[0, 0:TILE].astype(F32)
    for chip in range(1, CHIPS):
        total = total + got[chip, 0:TILE].astype(F32)
    total = total.astype(BF16)
    line, _ = row_col(16, TILE)
    lines = jnp.zeros((16, TILE), F32)
    slots = []
    for i in range(2):
        owner = owners[column, i]
        chip = owner // 2
        side = owner % 2
        slots.append(got[chip, pl.ds(pl.multiple_of(TILE + SLOT * side, SLOT), SLOT)])
        rows = got[chip, SECOND:].astype(F32)
        for k in range(2):
            pick = jnp.where(side == 0, rows[k : k + 1], rows[2 + k : 3 + k])
            lines = jnp.where(line == 8 * i + k, pick, lines)
    diagonals[...] = lines
    for chip in range(CHIPS):
        out[chip, 0:TILE] = total
        for i in range(2):
            out[chip, TILE + SLOT * i : TILE + SLOT * (i + 1)] = slots[i]


def load_grad(source, grad):
    for chip in range(CHIPS):
        top = TILE * (chip % 4)
        left = TILE * (chip // 4)
        grad[top : top + TILE, left : left + TILE] = source[chip, 0:TILE]


def precondition(grad, left, right):
    return mm(mm(left, grad).astype(BF16), right)


def own_block(mine, left_root, right_root, rounded, squares, grad):
    rows = pl.ds(pl.multiple_of(core_of() * WIDTH, WIDTH), WIDTH)
    load_grad(mine, grad)
    raw = precondition(grad[...], left_root[rows, :], right_root[rows, :])
    rounded[...] = raw.astype(BF16)
    column = jnp.sum(raw * raw, axis=0, keepdims=True)
    filled = jnp.broadcast_to(jnp.sum(column, axis=1, keepdims=True), (1, TILE))
    for k in range(squares.shape[0]):
        squares[k] = filled


def powers(left_root, square, cube, square_buffer, cube_buffer, sems):
    copies = []
    for block in range(2):
        rows = slice(block * WIDTH, (block + 1) * WIDTH)
        left = left_root[rows, :]
        second = mm(left, left).astype(BF16)
        square_buffer[rows, :] = second
        cube_buffer[rows, :] = mm(left, second).astype(BF16)
        for k, (source, target) in enumerate(((square_buffer, square), (cube_buffer, cube))):
            copies.append(pltpu.make_async_copy(source.at[rows], target.at[rows], sems.at[2 * block + k]))
            copies[-1].start()
    for copy in copies:
        copy.wait()


def late(
    owners, mine, other, diagonals, left_hbm, right_hbm, square_hbm, cube_hbm, stats,
    rounded, new_root, new_stats,
    grad, left_root, right_part, square, cube, old_stats, sems,
):
    core = core_of()
    replica = lax.axis_index("dp")
    column = lax.axis_index("fsdp")
    rest = pl.ds(pl.multiple_of((1 - core) * WIDTH, WIDTH), WIDTH)
    copies = [
        pltpu.make_async_copy(left_hbm, left_root, sems.at[0]),
        pltpu.make_async_copy(right_hbm.at[rest], right_part, sems.at[1]),
        pltpu.make_async_copy(square_hbm, square, sems.at[2]),
        pltpu.make_async_copy(cube_hbm, cube, sems.at[3]),
        pltpu.make_async_copy(stats.at[0, 0], old_stats, sems.at[4]),
    ]
    for copy in copies:
        copy.start()
    owner_known = (owners[column, 0] == replica) | (owners[column, 1] == replica)
    row, col = row_col(HALF, HALF)

    @pl.when(jnp.logical_not(owner_known))
    def _():
        new_stats[...] = jnp.zeros_like(new_stats)

    for copy in copies[:2]:
        copy.wait()
    load_grad(other, grad)
    rounded[...] = precondition(grad[...], left_root[rest, :], right_part[...]).astype(BF16)
    for copy in copies[2:]:
        copy.wait()

    def one(block, source, first, second, loaded):
        rows = slice(block * WIDTH, (block + 1) * WIDTH)
        if not loaded:
            load_grad(source, grad)
        gram = lax.dot_general(
            grad[...], grad[...], (((1,), (1,)), ((), ())), preferred_element_type=F32
        )

        @pl.when(owners[column, block] == replica)
        def _():
            new_stats[0, 0] = BETA * old_stats[...] + (1.0 - BETA) * gram

        start = TILE + SLOT * block

        def panel(part, k):
            return part[4 * k : 4 * k + 4, start : start + SLOT].reshape(TILE, TILE)

        packed = [
            jnp.concatenate(
                [jnp.concatenate([panel(part, k), panel(part, k + 1)], axis=1) for part in (first, second)], axis=0
            ).astype(F32)
            for k in (0, 2)
        ]
        corner, both = packed
        corner_t = jnp.transpose(corner)
        both_t = jnp.transpose(both)
        diagonal = jnp.concatenate(
            [diagonals[8 * block : 8 * block + 1], diagonals[8 * block + 1 : 8 * block + 2]], axis=1
        )
        high = jnp.where(row <= col, both, both_t)
        low = jnp.where(row > col, both, jnp.where(row == col, diagonal, both_t))
        old = jnp.concatenate(
            [jnp.concatenate([high, corner], axis=1), jnp.concatenate([corner_t, low], axis=1)], axis=0
        )
        fresh = (BETA * old + (1.0 - BETA) * gram).astype(BF16)
        change = mm(cube[rows, :], mm(fresh, square[rows, :]).astype(BF16))
        new_root[rows, :] = (1.25 * left_root[rows, :].astype(F32) - 0.25 * change).astype(BF16)

    @pl.when(core == 0)
    def _():
        one(1, other, mine, other, True)
        one(0, mine, mine, other, False)

    @pl.when(core == 1)
    def _():
        one(0, other, other, mine, True)
        one(1, mine, other, mine, False)


def rescale(count):
    def body(own_every, other_every, own, other, update, buffer, sems):
        core = core_of()
        totals = []
        for every in (own_every, other_every):
            total = every[0]
            for k in range(1, every.shape[0]):
                total = total + every[k]
            totals.append(total)
        total = totals[0] + totals[1]
        scale = lax.rsqrt(total[:, 0:1] / count + EPSILON)
        copies = []
        for source, block in ((own, core), (other, 1 - core)):
            for start in range(0, WIDTH, TILE):
                k = len(copies)
                buffer[k] = (source[start : start + TILE].astype(F32) * scale).astype(BF16)
                to = update.at[pl.ds(pl.multiple_of(block * WIDTH + start, TILE), TILE)]
                copies.append(pltpu.make_async_copy(buffer.at[k], to, sems.at[k]))
                copies[-1].start()
        for copy in copies:
            copy.wait()

    return body


def local(grads, stats, left_root, right_root, owners):
    n_fsdp = lax.axis_size("fsdp")
    rows = left_root.shape[0]
    same_core = [[2 * k + core for k in range(CHIPS)] for core in range(2)]
    swap = [(k, k ^ 1) for k in range(N_DP)]
    shape = jax.ShapeDtypeStruct
    product = 2 * WIDTH**3
    vmem = pltpu.VMEM
    grads, stats = [pltpu.with_memory_space_constraint(array, pltpu.HBM) for array in (grads, stats)]
    block = vmem((WIDTH, WIDTH), BF16)
    packed = WIDTH + TILE + 16

    send, keep = call(
        pack,
        [grads, stats],
        [shape((packed, WIDTH), BF16), shape((packed, WIDTH), BF16)],
        1 << 20,
        [vmem((HALF, WIDTH), F32), vmem((HALF, HALF), F32), pltpu.SemaphoreType.DMA((7,))],
        [pltpu.HBM, pltpu.HBM],
    )
    got = lax.ppermute(send, "dp", swap)
    (payload,) = call(pair_add, [keep, got], [shape((CHIPS, FIRST, TILE), BF16)], 1 << 20)
    arrived = exchange(payload, "dp", same_core)
    whole = shape((rows, WIDTH), BF16)
    square, cube = call(
        powers,
        [left_root],
        [whole, whole],
        4 * product,
        [vmem((rows, WIDTH), BF16), vmem((rows, WIDTH), BF16), pltpu.SemaphoreType.DMA((4,))],
        out_spaces=[pltpu.HBM, pltpu.HBM],
    )
    arrived, square, cube = lax.optimization_barrier((arrived, square, cube))
    repeated, diagonals = call(
        gather_sum,
        [owners, arrived],
        [shape((CHIPS, SECOND, TILE), BF16), shape((16, TILE), F32)],
        1 << 20,
        spaces=[pltpu.SMEM, vmem],
    )
    mine = exchange(repeated, "dp", same_core)
    own_rounded, squares = call(
        own_block,
        [mine, left_root, right_root],
        [shape((WIDTH, WIDTH), BF16), shape((n_fsdp, 1, TILE), F32)],
        2 * product,
        [block],
    )
    own_every = exchange(squares, "fsdp")
    after, _ = lax.optimization_barrier((mine, squares))
    other = lax.ppermute(after, "dp", swap)
    left_hbm, right_hbm, square, cube = [
        pltpu.with_memory_space_constraint(array, pltpu.HBM) for array in (left_root, right_root, square, cube)
    ]
    other_rounded, new_root, new_stats = call(
        late,
        [owners, mine, other, diagonals, left_hbm, right_hbm, square, cube, stats],
        [shape((WIDTH, WIDTH), BF16), whole, shape((1, 1, WIDTH, WIDTH), F32)],
        8 * product,
        [
            block,
            vmem((rows, WIDTH), BF16),
            block,
            vmem((rows, WIDTH), BF16),
            vmem((rows, WIDTH), BF16),
            vmem((WIDTH, WIDTH), F32),
            pltpu.SemaphoreType.DMA((5,)),
        ],
        [pltpu.SMEM, vmem, vmem, vmem] + [pltpu.HBM] * 5,
    )
    own_every, other_rounded, new_root = lax.optimization_barrier((own_every, other_rounded, new_root))
    other_every = lax.ppermute(own_every, "dp", swap)
    (update,) = call(
        rescale(float(rows * WIDTH * n_fsdp)),
        [own_every, other_every, own_rounded, other_rounded],
        [shape((rows, WIDTH), BF16)],
        1 << 20,
        [vmem((8, TILE, WIDTH), BF16), pltpu.SemaphoreType.DMA((8,))],
        out_spaces=[pltpu.HBM],
    )
    return (update, new_stats, new_root)


def solution(mesh):
    in_specs = (
        P("dp", None, "fsdp"),
        P("dp", "fsdp", None, None),
        P(None, "fsdp"),
        P(None, "fsdp"),
        P(),
    )
    out_specs = (P(None, "fsdp"), P("dp", "fsdp", None, None), P(None, "fsdp"))
    return jax.shard_map(local, mesh=mesh, in_specs=in_specs, out_specs=out_specs, check_vma=False)
```

```python
import jax
import jax.numpy as jnp
from jax import lax
from jax.experimental import pallas as pl
from jax.experimental.pallas import tpu as pltpu
from jax.sharding import PartitionSpec as P

BETA = 0.95
EPSILON = 1e-06
F32 = jnp.float32
BF16 = jnp.bfloat16

WIDTH = 512
HALF = 256
TILE = 128
SLOT = 32
CHIPS = 16
N_DP = 32
FIRST = TILE + 2 * SLOT + 8
SECOND = TILE + 2 * SLOT


def exchange(array, axis, groups=None):
    return lax.all_to_all(array, axis, 0, 0, axis_index_groups=groups)


def mm(left_arg, right_arg):
    return jnp.dot(left_arg, right_arg, preferred_element_type=F32)


def row_col(rows, cols):
    shape = (rows, cols)
    return lax.broadcasted_iota(jnp.int32, shape, 0), lax.broadcasted_iota(jnp.int32, shape, 1)


def core_of():
    return lax.rem(lax.axis_index("dp"), 2)


def call(body, args, outs, flops, scratch=(), spaces=None, out_spaces=None):
    spaces = spaces or [pltpu.VMEM] * len(args)
    out_spaces = out_spaces or [pltpu.VMEM] * len(outs)
    moved = sum(a.size * a.dtype.itemsize for a in args) + sum(o.size * o.dtype.itemsize for o in outs)
    return pl.pallas_call(
        body,
        out_shape=outs,
        in_specs=[pl.BlockSpec(memory_space=space) for space in spaces],
        out_specs=[pl.BlockSpec(memory_space=space) for space in out_spaces],
        scratch_shapes=scratch,
        cost_estimate=pl.CostEstimate(flops=flops, bytes_accessed=moved, transcendentals=0),
        compiler_params=pltpu.CompilerParams(vmem_limit_bytes=16 << 20),
    )(*args)


def pack(grads, stats, send, keep, upper, lower, sems):
    core = core_of()
    other = 1 - core
    copies = [
        pltpu.make_async_copy(stats.at[0, 0, 0:TILE], upper.at[0:TILE], sems.at[0]),
        pltpu.make_async_copy(stats.at[0, 0, TILE:HALF], upper.at[TILE:HALF], sems.at[1]),
        pltpu.make_async_copy(stats.at[0, 0, HALF:, HALF:], lower, sems.at[2]),
    ]
    for part in range(2):
        for k, (block, target) in enumerate(((other, send), (core, keep))):
            source = grads.at[0, pl.ds(pl.multiple_of(block * WIDTH + part * HALF, HALF), HALF)]
            copies.append(
                pltpu.make_async_copy(source, target.at[part * HALF : part * HALF + HALF], sems.at[3 + 2 * part + k])
            )
    for copy in copies:
        copy.start()
    for copy in copies[:3]:
        copy.wait()
    row, col = row_col(HALF, HALF)
    low = lower[...]
    both = jnp.where(row <= col, upper[:, :HALF], low).astype(BF16)
    corner = upper[:, HALF:].astype(BF16)
    diagonal = jnp.sum(jnp.where(row == col, low, 0.0), axis=0, keepdims=True)
    line, _ = row_col(16, TILE)
    lines = jnp.where(line == 2 * core, diagonal[:, :TILE], jnp.where(line == 2 * core + 1, diagonal[:, TILE:], 0.0))
    lines = lines.astype(BF16)
    end = WIDTH + TILE

    @pl.when(core == 0)
    def _():
        keep[WIDTH:end, :HALF] = corner[:TILE]
        keep[WIDTH:end, HALF:] = both[:TILE]
        send[WIDTH:end, :HALF] = corner[TILE:]
        send[WIDTH:end, HALF:] = both[TILE:]

    @pl.when(core == 1)
    def _():
        keep[WIDTH:end, :HALF] = corner[TILE:]
        keep[WIDTH:end, HALF:] = both[TILE:]
        send[WIDTH:end, :HALF] = corner[:TILE]
        send[WIDTH:end, HALF:] = both[:TILE]

    for start in range(0, WIDTH, TILE):
        keep[end:, start : start + TILE] = lines
        send[end:, start : start + TILE] = lines
    for copy in copies[3:]:
        copy.wait()


def pair_add(keep, got, out):
    core = core_of()
    mine = pl.multiple_of(TILE + SLOT * core, SLOT)
    theirs = pl.multiple_of(TILE + SLOT * (1 - core), SLOT)
    lines = (keep[WIDTH + TILE :, :TILE].astype(F32) + got[WIDTH + TILE :, :TILE].astype(F32))[0:8].astype(BF16)
    for chip in range(CHIPS):
        cols = slice(TILE * (chip // 4), TILE * (chip // 4) + TILE)
        top = TILE * (chip % 4)
        own = keep[top : top + TILE, cols].astype(F32)
        out[chip, 0:TILE] = (own + got[top : top + TILE, cols].astype(F32)).astype(BF16)
        at = WIDTH + SLOT * (chip % 4)
        out[chip, pl.ds(mine, SLOT)] = keep[at : at + SLOT, cols]
        out[chip, pl.ds(theirs, SLOT)] = got[at : at + SLOT, cols]
        out[chip, SECOND:] = lines


def gather_sum(owners, got, out, diagonals):
    column = lax.axis_index("fsdp")
    total = got[0, 0:TILE].astype(F32)
    for chip in range(1, CHIPS):
        total = total + got[chip, 0:TILE].astype(F32)
    total = total.astype(BF16)
    line, _ = row_col(16, TILE)
    lines = jnp.zeros((16, TILE), F32)
    slots = []
    for i in range(2):
        owner = owners[column, i]
        chip = owner // 2
        side = owner % 2
        slots.append(got[chip, pl.ds(pl.multiple_of(TILE + SLOT * side, SLOT), SLOT)])
        rows = got[chip, SECOND:].astype(F32)
        for k in range(2):
            pick = jnp.where(side == 0, rows[k : k + 1], rows[2 + k : 3 + k])
            lines = jnp.where(line == 8 * i + k, pick, lines)
    diagonals[...] = lines
    for chip in range(CHIPS):
        out[chip, 0:TILE] = total
        for i in range(2):
            out[chip, TILE + SLOT * i : TILE + SLOT * (i + 1)] = slots[i]


def load_grad(source, grad):
    for chip in range(CHIPS):
        top = TILE * (chip % 4)
        left = TILE * (chip // 4)
        grad[top : top + TILE, left : left + TILE] = source[chip, 0:TILE]


def precondition(source, left_root, right_root, rounded, grad, block):
    rows = pl.ds(pl.multiple_of(block * WIDTH, WIDTH), WIDTH)
    load_grad(source, grad)
    product = mm(left_root[rows, :], grad[...]).astype(BF16)
    raw = mm(product, right_root[rows, :])
    rounded[...] = raw.astype(BF16)
    column = jnp.sum(raw * raw, axis=0, keepdims=True)
    return jnp.sum(column, axis=1, keepdims=True)


def own_block(mine, left_root, right_root, rounded, squares, grad):
    total = precondition(mine, left_root, right_root, rounded, grad, core_of())
    squares[...] = jnp.broadcast_to(total, squares.shape)


def other_block(other, left_root, right_root, own, rounded, squares, grad):
    total = precondition(other, left_root, right_root, rounded, grad, 1 - core_of())
    filled = own[0:1] + jnp.broadcast_to(total, (1, TILE))
    for k in range(squares.shape[0]):
        squares[k] = filled


def powers(left_root, square, cube, square_buffer, cube_buffer, sems):
    copies = []
    for block in range(2):
        rows = slice(block * WIDTH, (block + 1) * WIDTH)
        left = left_root[rows, :]
        second = mm(left, left).astype(BF16)
        square_buffer[rows, :] = second
        cube_buffer[rows, :] = mm(left, second).astype(BF16)
        for k, (source, target) in enumerate(((square_buffer, square), (cube_buffer, cube))):
            copies.append(pltpu.make_async_copy(source.at[rows], target.at[rows], sems.at[2 * block + k]))
            copies[-1].start()
    for copy in copies:
        copy.wait()


def newton(
    owners, mine_hbm, other_hbm, diagonals, left_hbm, square_hbm, cube_hbm, stats, squares,
    new_root, new_stats,
    grad, left_root, square, cube, mine, other, old_stats, sems,
):
    core = core_of()
    replica = lax.axis_index("dp")
    column = lax.axis_index("fsdp")
    copies = [
        pltpu.make_async_copy(source, target, sems.at[k])
        for k, (source, target) in enumerate(
            (
                (mine_hbm, mine),
                (other_hbm, other),
                (stats.at[0, 0], old_stats),
                (square_hbm, square),
                (cube_hbm, cube),
                (left_hbm, left_root),
            )
        )
    ]
    for copy in copies:
        copy.start()
    owner_known = (owners[column, 0] == replica) | (owners[column, 1] == replica)
    row, col = row_col(HALF, HALF)

    @pl.when(jnp.logical_not(owner_known))
    def _():
        new_stats[...] = jnp.zeros_like(new_stats)

    for copy in copies[:2]:
        copy.wait()

    def one(block, source, first, second, pending):
        rows = slice(block * WIDTH, (block + 1) * WIDTH)
        load_grad(source, grad)
        gram = lax.dot_general(
            grad[...], grad[...], (((1,), (1,)), ((), ())), preferred_element_type=F32
        )
        for copy in pending:
            copy.wait()

        @pl.when(owners[column, block] == replica)
        def _():
            new_stats[0, 0] = BETA * old_stats[...] + (1.0 - BETA) * gram

        start = TILE + SLOT * block

        def panel(part, k):
            return part[4 * k : 4 * k + 4, start : start + SLOT].reshape(TILE, TILE)

        packed = [
            jnp.concatenate(
                [jnp.concatenate([panel(part, k), panel(part, k + 1)], axis=1) for part in (first, second)], axis=0
            ).astype(F32)
            for k in (0, 2)
        ]
        corner, both = packed
        corner_t = jnp.transpose(corner)
        both_t = jnp.transpose(both)
        diagonal = jnp.concatenate(
            [diagonals[8 * block : 8 * block + 1], diagonals[8 * block + 1 : 8 * block + 2]], axis=1
        )
        high = jnp.where(row <= col, both, both_t)
        low = jnp.where(row > col, both, jnp.where(row == col, diagonal, both_t))
        old = jnp.concatenate(
            [jnp.concatenate([high, corner], axis=1), jnp.concatenate([corner_t, low], axis=1)], axis=0
        )
        fresh = (BETA * old + (1.0 - BETA) * gram).astype(BF16)
        change = mm(cube[rows, :], mm(fresh, square[rows, :]).astype(BF16))
        new_root[rows, :] = (1.25 * left_root[rows, :].astype(F32) - 0.25 * change).astype(BF16)

    @pl.when(core == 0)
    def _():
        one(0, mine, mine, other, copies[2:])
        one(1, other, mine, other, [])

    @pl.when(core == 1)
    def _():
        one(0, other, other, mine, copies[2:])
        one(1, mine, other, mine, [])


def rescale(count):
    def body(every, own, other, update, buffer, sems):
        core = core_of()
        total = every[0]
        for k in range(1, every.shape[0]):
            total = total + every[k]
        scale = lax.rsqrt(total[:, 0:1] / count + EPSILON)
        copies = []
        for source, block in ((own, core), (other, 1 - core)):
            for start in range(0, WIDTH, TILE):
                k = len(copies)
                buffer[k] = (source[start : start + TILE].astype(F32) * scale).astype(BF16)
                to = update.at[pl.ds(pl.multiple_of(block * WIDTH + start, TILE), TILE)]
                copies.append(pltpu.make_async_copy(buffer.at[k], to, sems.at[k]))
                copies[-1].start()
        for copy in copies:
            copy.wait()

    return body


def local(grads, stats, left_root, right_root, owners):
    n_fsdp = lax.axis_size("fsdp")
    rows = left_root.shape[0]
    same_core = [[2 * k + core for k in range(CHIPS)] for core in range(2)]
    swap = [(k, k ^ 1) for k in range(N_DP)]
    shape = jax.ShapeDtypeStruct
    product = 2 * WIDTH**3
    vmem = pltpu.VMEM
    grads, stats = [pltpu.with_memory_space_constraint(array, pltpu.HBM) for array in (grads, stats)]
    block = vmem((WIDTH, WIDTH), BF16)
    packed = WIDTH + TILE + 16

    send, keep = call(
        pack,
        [grads, stats],
        [shape((packed, WIDTH), BF16), shape((packed, WIDTH), BF16)],
        1 << 20,
        [vmem((HALF, WIDTH), F32), vmem((HALF, HALF), F32), pltpu.SemaphoreType.DMA((7,))],
        [pltpu.HBM, pltpu.HBM],
    )
    got = lax.ppermute(send, "dp", swap)
    (payload,) = call(pair_add, [keep, got], [shape((CHIPS, FIRST, TILE), BF16)], 1 << 20)
    arrived = exchange(payload, "dp", same_core)
    whole = shape((rows, WIDTH), BF16)
    square, cube = call(
        powers,
        [left_root],
        [whole, whole],
        4 * product,
        [vmem((rows, WIDTH), BF16), vmem((rows, WIDTH), BF16), pltpu.SemaphoreType.DMA((4,))],
        out_spaces=[pltpu.HBM, pltpu.HBM],
    )
    arrived, square, cube = lax.optimization_barrier((arrived, square, cube))
    repeated, diagonals = call(
        gather_sum,
        [owners, arrived],
        [shape((CHIPS, SECOND, TILE), BF16), shape((16, TILE), F32)],
        1 << 20,
        spaces=[pltpu.SMEM, vmem],
    )
    mine = exchange(repeated, "dp", same_core)
    other = lax.ppermute(mine, "dp", swap)
    own_rounded, own_squares = call(
        own_block,
        [mine, left_root, right_root],
        [shape((WIDTH, WIDTH), BF16), shape((8, TILE), F32)],
        2 * product,
        [block],
    )
    other_rounded, squares = call(
        other_block,
        [other, left_root, right_root, own_squares],
        [shape((WIDTH, WIDTH), BF16), shape((n_fsdp, 1, TILE), F32)],
        2 * product,
        [block],
    )
    every = exchange(squares, "fsdp")
    left_hbm, square, cube, mine_hbm, other_hbm = [
        pltpu.with_memory_space_constraint(array, pltpu.HBM) for array in (left_root, square, cube, mine, other)
    ]
    table = vmem((rows, WIDTH), BF16)
    new_root, new_stats = call(
        newton,
        [owners, mine_hbm, other_hbm, diagonals, left_hbm, square, cube, stats, squares],
        [whole, shape((1, 1, WIDTH, WIDTH), F32)],
        6 * product,
        [
            block,
            table,
            table,
            table,
            vmem((CHIPS, SECOND, TILE), BF16),
            vmem((CHIPS, SECOND, TILE), BF16),
            vmem((WIDTH, WIDTH), F32),
            pltpu.SemaphoreType.DMA((6,)),
        ],
        [pltpu.SMEM, pltpu.HBM, pltpu.HBM, vmem] + [pltpu.HBM] * 4 + [vmem],
    )
    (update,) = call(
        rescale(float(rows * WIDTH * n_fsdp)),
        [every, own_rounded, other_rounded],
        [shape((rows, WIDTH), BF16)],
        1 << 20,
        [vmem((8, TILE, WIDTH), BF16), pltpu.SemaphoreType.DMA((8,))],
        out_spaces=[pltpu.HBM],
    )
    return (update, new_stats, new_root)


def solution(mesh):
    in_specs = (
        P("dp", None, "fsdp"),
        P("dp", "fsdp", None, None),
        P(None, "fsdp"),
        P(None, "fsdp"),
        P(),
    )
    out_specs = (P(None, "fsdp"), P("dp", "fsdp", None, None), P(None, "fsdp"))
    return jax.shard_map(local, mesh=mesh, in_specs=in_specs, out_specs=out_specs, check_vma=False)
```
